1024 devices in a mesh: dcn: 8 (over y, x_lo), ctx: 32 (over z), head: 4 (over x_hi, core).
Axes of the slice: x: 4 (x_hi: 2, x_lo: 2; x = x_hi * 2 + x_lo), y: 4, z: 32, core: 2. Of those that a mesh axis runs over, the one named last changes fastest.
Arguments:
- queries: bfloat16 [65536, 64, 128], P(('dcn', 'ctx'), 'head'), may hold values from -26 to 26
- keys: bfloat16 [65536, 8, 128], P(('dcn', 'ctx'), 'head'), may hold values from -6 to 6
- values: bfloat16 [65536, 8, 128], P(('dcn', 'ctx'), 'head'), may hold values from -6 to 6
- seg_ids: int32 [65536], P(('dcn', 'ctx')), may hold values from 0 to 255, never falling along the last dimension, each value on 1 to 768 neighbouring positions
Outputs:
- attended: bfloat16 [65536, 64, 128], P(('dcn', 'ctx'), 'head')
The draws below stay inside these ranges and needn't reach their ends.
Inputs may be any that keep to these rules, and one draw needn't show every extreme that they name: `seg_ids`: ids never fall along the sequence; every document has 1 to 768 tokens and one has exactly 768.
All inputs are finite; a program needn't handle non-finite values.
Results may differ from the reference program's by a relative error of at most 0.0025.
Values may be sent and summed in bfloat16 or wider, within the bound.
No kernel may reach another device: no remote copies, remote signals or barrier semaphores. Data moves between devices by JAX's collectives and lax.ppermute only.
A program may use at most 32 MiB of HBM per device.

```python
import math
import jax
import jax.numpy as jnp
import numpy as np
from jax import lax

HD = 128
HEADS = 64
KV_HEADS = 8
STEPS = 3
TOK_DEV = 256
TOKENS = 65536
DOC_MAX = 768
NDOCS = 256


def paired_fields(key):
    base = jax.random.fold_in(key, 11)
    key_field = jnp.clip(jax.random.normal(jax.random.fold_in(base, 1), (TOKENS, KV_HEADS, HD), jnp.float32), -4.0, 4.0) * 1.5
    query_field = jnp.clip(jax.random.normal(jax.random.fold_in(base, 2), (TOKENS, HEADS, HD), jnp.float32), -4.0, 4.0) * 2.0
    return (query_field.astype(jnp.bfloat16), key_field.astype(jnp.bfloat16))


def draw_queries(key, part):
    return paired_fields(key)[0]


def draw_keys(key, part):
    return paired_fields(key)[1]


def level_of(rng, dims, pieces, smallest, top_value):
    loudness, own = 1.0, jax.random.fold_in(rng, 6)
    for position, blocks in pieces:
        steps = jnp.exp(jax.random.uniform(jax.random.fold_in(own, position), (blocks,), jnp.float32, smallest / len(pieces), top_value / len(pieces)))
        loudness = loudness * jnp.repeat(steps, dims[position] // blocks).reshape([-1 if axis == position else 1 for axis in range(len(dims))])
    return loudness


def profile(amount, total, most, slope):
    loads = [(1 << 20) // math.isqrt(rank ** slope) + 1 for rank in range(2, amount + 1)]
    spare, counts = total - most - (amount - 1), [1] * (amount - 1)
    while spare > 0:
        candidates = [i for i in range(amount - 1) if counts[i] < most]
        mass, budget = sum([loads[i] for i in candidates]), spare
        for i in candidates:
            extra = min(most - counts[i], max(1, budget * loads[i] // mass), spare)
            counts[i] = counts[i] + extra
            spare = spare - extra
    return np.array([most] + counts)


def uneven(own_key, number_of, total, most, slope):
    if number_of == 2:
        one = jax.random.randint(own_key, (), max(1, total - most), min(most, total - 1) + 1)
        return jnp.stack([one, total - one])
    sizes = jnp.asarray(profile(number_of, total, most, slope), jnp.int32)
    twos = (number_of - 1) // 2
    donor, receiver = sizes[1:1 + 2 * twos:2], sizes[2:2 + 2 * twos:2]
    slack = jnp.minimum(donor - 1, most - receiver)
    passed = jax.random.randint(jax.random.fold_in(own_key, 1), (twos,), 0, 1 << 20) % (slack + 1)
    sizes = sizes.at[1:1 + 2 * twos:2].set(donor - passed).at[2:2 + 2 * twos:2].set(receiver + passed)
    return sizes[jax.random.permutation(jax.random.fold_in(own_key, 2), number_of)]


def gaussian(rng, extent, width, bound, pieces=(), held_as=jnp.bfloat16):
    array = width * jax.random.normal(rng, extent, jnp.float32)
    if pieces:
        array = array * level_of(rng, extent, pieces, -0.22, 0.18)
    return jnp.clip(array, -bound, bound).astype(held_as)


def setup_inputs(seed: int = 0) -> dict:
    streams_of = jax.random.split(jax.random.key(seed), 5)
    return {
        "queries": draw_queries(jax.random.fold_in(streams_of[4], 71), 0),
        "keys": draw_keys(jax.random.fold_in(streams_of[4], 71), 0),
        "values": gaussian(streams_of[2], (TOKENS, KV_HEADS, HD), 1.0, 6.0, ((0, 256), (1, 4))),
        "seg_ids": jnp.searchsorted(jnp.cumsum(uneven(streams_of[3], NDOCS, TOKENS, DOC_MAX, 2)), jnp.arange(TOKENS), side="right").astype(jnp.int32),
    }


def reference(queries, keys, values, seg_ids):
    group_size = HEADS // KV_HEADS
    reach = STEPS * TOK_DEV
    window = (STEPS + 1) * TOK_DEV
    key_pad = jnp.concatenate([jnp.zeros((reach, KV_HEADS, HD), jnp.float32), keys.astype(jnp.float32)], axis=0)
    val_pad = jnp.concatenate([jnp.zeros((reach, KV_HEADS, HD), jnp.float32), values.astype(jnp.float32)], axis=0)
    seg_pad = jnp.concatenate([jnp.full((reach,), -1, jnp.int32), seg_ids.astype(jnp.int32)], axis=0)
    tile_count = TOKENS // TOK_DEV

    def one_tile(index):
        first = (index * TOK_DEV).astype(jnp.int32)
        query_tile = lax.dynamic_slice_in_dim(queries, first, TOK_DEV, 0).astype(jnp.float32)
        query_seg = lax.dynamic_slice_in_dim(seg_ids, first, TOK_DEV, 0)
        key_win = lax.dynamic_slice_in_dim(key_pad, first, window, 0)
        val_win = lax.dynamic_slice_in_dim(val_pad, first, window, 0)
        seg_win = lax.dynamic_slice_in_dim(seg_pad, first, window, 0)
        query_pos = first + jnp.arange(TOK_DEV, dtype=jnp.int32)
        key_pos = first - reach + jnp.arange(window, dtype=jnp.int32)
        mask = (query_seg[:, None] == seg_win[None, :]) & (key_pos[None, :] <= query_pos[:, None])
        grouped = query_tile.reshape(TOK_DEV, KV_HEADS, group_size, HD)
        scores = jnp.einsum("qkgd,skd->kgqs", grouped, key_win) * (HD ** -0.5)
        scores = jnp.where(mask, scores, -1e30)
        top = jnp.max(scores, axis=-1, keepdims=True)
        weights = jnp.where(mask, jnp.exp(scores - top), 0.0)
        total = jnp.sum(weights, axis=-1)
        rounded = lax.optimization_barrier(weights.astype(jnp.bfloat16)).astype(jnp.float32)
        summed = jnp.einsum("kgqs,skd->kgqd", rounded, val_win)
        result = summed / total[..., None]
        return result.transpose(2, 0, 1, 3).reshape(TOK_DEV, HEADS, HD).astype(jnp.bfloat16)

    tiles = lax.map(one_tile, jnp.arange(tile_count, dtype=jnp.int32))
    return tiles.reshape(TOKENS, HEADS, HD)
```

```python
import jax
import jax.numpy as jnp
from jax import lax
from jax.experimental import pallas as pl
from jax.experimental.pallas import tpu as pltpu
from jax.sharding import PartitionSpec as P


AXES = ("dcn", "ctx")
LOG2E = 1.4426950408889634
NEG = -1e30
CHUNK = 32
LIMIT = 24 * 1024 * 1024

VMEM = pl.BlockSpec(memory_space=pltpu.VMEM)


def passed_along(x, by):
    count = lax.axis_size(AXES)
    pairs = [(i, i + by) for i in range(count) if 0 <= i + by < count]
    return lax.ppermute(x, AXES, pairs)


def pack_keys(k_ref, seg_ref, out_ref):
    tok, kv, _ = k_ref.shape
    keys = k_ref[...].astype(jnp.float32)
    for g in range(kv):
        out_ref[g * tok : (g + 1) * tok, :] = keys[:, g, :].astype(jnp.bfloat16)
    rows = seg_ref.shape[0]
    marks = (seg_ref[...] + 1).astype(jnp.float32)
    pad = jnp.zeros((8 - rows, 128), jnp.float32)
    out_ref[kv * tok :, :] = jnp.concatenate([marks, pad], axis=0).astype(jnp.bfloat16)


def pack_values(v_ref, out_ref):
    tok, kv, _ = v_ref.shape
    vals = v_ref[...].astype(jnp.float32)
    for g in range(kv):
        out_ref[g * tok : (g + 1) * tok, :] = vals[:, g, :].astype(jnp.bfloat16)


def dot_t(a, b):
    return lax.dot_general(a, b, (((1,), (1,)), ((), ())), preferred_element_type=jnp.float32)


def with_ones(vals):
    return jnp.concatenate([vals, jnp.ones(vals.shape, vals.dtype)], axis=1)


def queries_of(q_ref, t0, g, group):
    q = q_ref[pl.ds(t0, CHUNK), :, :].astype(jnp.float32)
    hd = q.shape[-1]
    return q[:, g * group : (g + 1) * group, :].reshape(CHUNK * group, hd).astype(jnp.bfloat16)


def key_marks(k_ref, tok):
    rows = tok // 128
    base = k_ref.shape[0] - 8
    tail = k_ref[base : base + 8, :].astype(jnp.float32)
    return jnp.concatenate([tail[r : r + 1, :] for r in range(rows)], axis=1)


def own_tile(q_ref, k_ref, v_ref, acc_ref, top_ref, bias_ref):
    tok, heads, hd = q_ref.shape
    kv = acc_ref.shape[0]
    group = heads // kv
    scale = hd**-0.5 * LOG2E
    key_seg = key_marks(k_ref, tok)
    for r in range(tok // 128):
        marks = jnp.broadcast_to(key_seg[:, r * 128 : (r + 1) * 128], (128, 128)).T
        row = lax.broadcasted_iota(jnp.int32, (128, tok), 0) + r * 128
        col = lax.broadcasted_iota(jnp.int32, (128, tok), 1)
        same = jnp.concatenate([marks] * (tok // 128), axis=1) == key_seg
        bias_ref[r * 128 : (r + 1) * 128, :] = jnp.where(same & (col <= row), 0.0, NEG)
    for c in range(tok // CHUNK):
        t0 = c * CHUNK
        width = min(tok, -(-(t0 + CHUNK) // 128) * 128)
        bias = bias_ref[t0 : t0 + CHUNK, :width]
        for g in range(kv):
            scores = dot_t(queries_of(q_ref, t0, g, group), k_ref[g * tok : g * tok + width, :])
            scores = (scores.reshape(CHUNK, group, width) + bias[:, None, :]).reshape(CHUNK * group, width)
            top = jnp.max(scores, axis=1, keepdims=True)
            weights = jnp.exp2((scores - top) * scale).astype(jnp.bfloat16)
            rows = pl.ds(t0 * group, CHUNK * group)
            acc_ref[g, rows, :] = jnp.dot(
                weights, with_ones(v_ref[g * tok : g * tok + width, :]), preferred_element_type=jnp.float32
            )
            top_ref[g, rows, :] = jnp.broadcast_to(top, (CHUNK * group, 128))


def reach_of(k_ref, seg_ref, tok):
    marks = (seg_ref[...] + 1).astype(jnp.float32)
    first = marks[0:1, 0:1]
    usable = key_marks(k_ref, tok) == first
    reach = jnp.sum(jnp.where(marks == first, 1.0, 0.0)).astype(jnp.int32)
    any_key = jnp.max(jnp.where(usable, 1.0, 0.0)) > 0.5
    chunks = jnp.where(any_key, (reach + CHUNK - 1) // CHUNK, 0)
    return usable, reach, chunks


def next_tile(q_ref, k_ref, v_ref, seg_ref, acc_in, top_in, acc_ref, top_ref):
    tok, heads, hd = q_ref.shape
    kv = acc_ref.shape[0]
    group = heads // kv
    scale = hd**-0.5 * LOG2E
    usable, reach, chunks = reach_of(k_ref, seg_ref, tok)
    token = lax.broadcasted_iota(jnp.int32, (CHUNK * group, tok), 0) // group

    def body(c, _):
        t0 = pl.multiple_of(c * CHUNK, CHUNK)
        mask = usable & (token + t0 < reach)
        for g in range(kv):
            rows = pl.ds(pl.multiple_of(t0 * group, CHUNK * group), CHUNK * group)
            scores = dot_t(queries_of(q_ref, t0, g, group), k_ref[g * tok : (g + 1) * tok, :])
            scores = jnp.where(mask, scores, NEG)
            old = top_ref[g, rows, :]
            top = jnp.maximum(old, jnp.max(scores, axis=1, keepdims=True))
            weights = jnp.exp2((scores - top[:, :1]) * scale).astype(jnp.bfloat16)
            shrink = jnp.exp2((old - top) * scale)
            update = jnp.dot(
                weights, with_ones(v_ref[g * tok : (g + 1) * tok, :]), preferred_element_type=jnp.float32
            )
            acc_ref[g, rows, :] = acc_ref[g, rows, :] * jnp.concatenate([shrink, shrink], axis=1) + update
            top_ref[g, rows, :] = top
        return 0

    lax.fori_loop(0, chunks, body, 0)


def last_weights(q_ref, k_ref, seg_ref, acc_in, top_ref, acc_ref, w_ref):
    tok, heads, hd = q_ref.shape
    kv = acc_ref.shape[0]
    group = heads // kv
    scale = hd**-0.5 * LOG2E
    usable, reach, chunks = reach_of(k_ref, seg_ref, tok)
    token = lax.broadcasted_iota(jnp.int32, (CHUNK * group, tok), 0) // group

    def body(c, _):
        t0 = pl.multiple_of(c * CHUNK, CHUNK)
        mask = usable & (token + t0 < reach)
        for g in range(kv):
            rows = pl.ds(pl.multiple_of(t0 * group, CHUNK * group), CHUNK * group)
            scores = dot_t(queries_of(q_ref, t0, g, group), k_ref[g * tok : (g + 1) * tok, :])
            scores = jnp.where(mask, scores, NEG)
            old = top_ref[g, rows, :]
            top = jnp.maximum(old, jnp.max(scores, axis=1, keepdims=True))
            w_ref[g, rows, :] = jnp.exp2((scores - top[:, :1]) * scale).astype(jnp.bfloat16)
            shrink = jnp.exp2((old - top) * scale)
            acc_ref[g, rows, :] = acc_ref[g, rows, :] * jnp.concatenate([shrink, shrink], axis=1)
        return 0

    lax.fori_loop(0, chunks, body, 0)


def last_values(k_ref, v_ref, seg_ref, w_ref, acc_ref, out_ref):
    tok, heads, hd = out_ref.shape
    kv = acc_ref.shape[0]
    group = heads // kv
    _, _, chunks = reach_of(k_ref, seg_ref, tok)

    def finish(t0, states):
        parts = [(s[:, :hd] / s[:, hd:]).reshape(CHUNK, group, hd) for s in states]
        out_ref[pl.ds(t0, CHUNK), :, :] = jnp.concatenate(parts, axis=1).astype(jnp.bfloat16)

    def with_last(c, _):
        t0 = pl.multiple_of(c * CHUNK, CHUNK)
        rows = pl.ds(pl.multiple_of(t0 * group, CHUNK * group), CHUNK * group)
        states = []
        for g in range(kv):
            update = jnp.dot(
                w_ref[g, rows, :], with_ones(v_ref[g * tok : (g + 1) * tok, :]), preferred_element_type=jnp.float32
            )
            states.append(acc_ref[g, rows, :] + update)
        finish(t0, states)
        return 0

    def without(c, _):
        t0 = pl.multiple_of(c * CHUNK, CHUNK)
        rows = pl.ds(pl.multiple_of(t0 * group, CHUNK * group), CHUNK * group)
        finish(t0, [acc_ref[g, rows, :] for g in range(kv)])
        return 0

    lax.fori_loop(0, chunks, with_last, 0)
    lax.fori_loop(chunks, tok // CHUNK, without, 0)


def kernel(body, outs, ins, aliases=None, scratch=()):
    return pl.pallas_call(
        body,
        out_shape=outs,
        in_specs=[VMEM] * ins,
        out_specs=jax.tree.map(lambda _: VMEM, outs),
        input_output_aliases=aliases or {},
        scratch_shapes=scratch,
        compiler_params=pltpu.CompilerParams(vmem_limit_bytes=LIMIT),
    )


def local(queries, keys, values, seg_ids):
    tok, heads, hd = queries.shape
    kv = keys.shape[1]
    group = heads // kv
    bf16, f32 = jnp.bfloat16, jnp.float32
    seg_rows = seg_ids.reshape(tok // 128, 128)
    acc_shape = jax.ShapeDtypeStruct((kv, tok * group, 2 * hd), f32)
    top_shape = jax.ShapeDtypeStruct((kv, tok * group, 128), f32)

    def hop(x):
        return passed_along(x, 1)

    k0 = kernel(pack_keys, jax.ShapeDtypeStruct((kv * tok + 8, hd), bf16), 2)(keys, seg_rows)
    v0 = kernel(pack_values, jax.ShapeDtypeStruct((kv * tok, hd), bf16), 1)(values)
    k1, v1 = hop(k0), hop(v0)
    k2, v2 = hop(k1), hop(v1)
    k3, v3 = hop(k2), hop(v2)
    acc, top = kernel(own_tile, (acc_shape, top_shape), 3, scratch=[pltpu.VMEM((tok, tok), f32)])(queries, k0, v0)
    for kd, vd in ((k1, v1), (k2, v2)):
        acc, top = kernel(next_tile, (acc_shape, top_shape), 6, {4: 0, 5: 1})(queries, kd, vd, seg_rows, acc, top)
    acc, weights = kernel(
        last_weights, (acc_shape, jax.ShapeDtypeStruct((kv, tok * group, tok), bf16)), 5, {3: 0}
    )(queries, k3, seg_rows, acc, top)
    return kernel(last_values, jax.ShapeDtypeStruct((tok, heads, hd), bf16), 5)(k3, v3, seg_rows, weights, acc)


def solution(mesh):
    placed = (
        P(AXES, "head", None),
        P(AXES, "head", None),
        P(AXES, "head", None),
        P(AXES),
    )
    return jax.shard_map(
        local,
        mesh=mesh,
        in_specs=placed,
        out_specs=P(AXES, "head", None),
        check_vma=False,
    )
```

```python
import jax
import jax.numpy as jnp
from jax import lax
from jax.experimental import pallas as pl
from jax.experimental.pallas import tpu as pltpu
from jax.sharding import PartitionSpec as P


AXES = ("dcn", "ctx")
LOG2E = 1.4426950408889634
NEG = -1e30
CHUNK = 64
HALF = 128
LIMIT = 24 * 1024 * 1024

VMEM = pl.BlockSpec(memory_space=pltpu.VMEM)
HBM = pl.BlockSpec(memory_space=pltpu.HBM)


def passed_along(x, by):
    count = lax.axis_size(AXES)
    pairs = [(i, i + by) for i in range(count) if 0 <= i + by < count]
    return lax.ppermute(x, AXES, pairs)


def prepare(k_hbm, v_hbm, seg_hbm, key_ref, val_ref, k_ref, v_ref, seg_ref, sems):
    tok, kv, _ = k_ref.shape
    rows = seg_ref.shape[0]
    copies = [
        pltpu.make_async_copy(src, dst, sems.at[n])
        for n, (src, dst) in enumerate(((k_hbm, k_ref), (seg_hbm, seg_ref), (v_hbm, v_ref)))
    ]
    for copy in copies:
        copy.start()

    def pack(src, dst):
        x = src[...].astype(jnp.float32)
        for g in range(kv):
            dst[g * tok : (g + 1) * tok, :] = x[:, g, :].astype(jnp.bfloat16)

    copies[0].wait()
    pack(k_ref, key_ref)
    copies[1].wait()
    marks = (seg_ref[...] + 1).astype(jnp.float32)
    pad = jnp.zeros((8 - rows, 128), jnp.float32)
    key_ref[kv * tok :, :] = jnp.concatenate([marks, pad], axis=0).astype(jnp.bfloat16)
    copies[2].wait()
    pack(v_ref, val_ref)


def wide(x, like):
    return jnp.concatenate([x] * (like.shape[1] // x.shape[1]), axis=1)


def dot_t(a, b):
    return lax.dot_general(a, b, (((1,), (1,)), ((), ())), preferred_element_type=jnp.float32)


def with_ones(vals):
    return jnp.concatenate([vals, jnp.ones(vals.shape, vals.dtype)], axis=1)


def marks_of(key_ref, tok):
    base = key_ref.shape[0] - 8
    tail = key_ref[base : base + 8, :].astype(jnp.float32)
    return jnp.concatenate([tail[r : r + 1, :] for r in range(tok // 128)], axis=1)


def own_tile(raw_ref, key_ref, val_ref, acc_ref, top_ref, q_ref, bias_ref):
    tok, heads, hd = raw_ref.shape
    kv = acc_ref.shape[0]
    group = heads // kv
    scale = hd**-0.5 * LOG2E
    key_seg = marks_of(key_ref, tok)
    for r in range(tok // 128):
        marks = jnp.broadcast_to(key_seg[:, r * 128 : (r + 1) * 128], (128, 128)).T
        row = lax.broadcasted_iota(jnp.int32, (128, tok), 0) + r * 128
        col = lax.broadcasted_iota(jnp.int32, (128, tok), 1)
        same = jnp.concatenate([marks] * (tok // 128), axis=1) == key_seg
        bias_ref[r * 128 : (r + 1) * 128, :] = jnp.where(same & (col <= row), 0.0, NEG)
    for c in range(tok // CHUNK):
        t0 = c * CHUNK
        width = min(tok, -(-(t0 + CHUNK) // 128) * 128)
        bias = bias_ref[t0 : t0 + CHUNK, :width]
        rows = slice(t0 * group, (t0 + CHUNK) * group)
        raw = raw_ref[t0 : t0 + CHUNK, :, :].astype(jnp.float32)
        for g in range(kv):
            q = raw[:, g * group : (g + 1) * group, :].reshape(CHUNK * group, hd).astype(jnp.bfloat16)
            q_ref[g, rows, :] = q
            scores = dot_t(q, key_ref[g * tok : g * tok + width, :])
            scores = (scores.reshape(CHUNK, group, width) + bias[:, None, :]).reshape(CHUNK * group, width)
            top = jnp.max(scores, axis=1, keepdims=True)
            weights = jnp.exp2((scores - top) * scale).astype(jnp.bfloat16)
            acc_ref[g, rows, :] = jnp.dot(
                weights, with_ones(val_ref[g * tok : g * tok + width, :]), preferred_element_type=jnp.float32
            )
            top_ref[g, rows, :] = jnp.broadcast_to(top, (CHUNK * group, 128))


def reach_of(own_ref, far_ref, tok):
    own = marks_of(own_ref, tok)
    first = own[:, 0:1]
    usable = marks_of(far_ref, tok) == first
    reach = jnp.sum(jnp.where(own == first, 1.0, 0.0)).astype(jnp.int32)
    found = jnp.sum(jnp.where(usable, 1.0, 0.0)).astype(jnp.int32)
    return usable, jnp.where(found > 0, reach, 0), found


def far_scores(q_ref, key_ref, g, rows, t0, reach, usable, lo, hi):
    tok = usable.shape[1]
    count = rows.stop - rows.start
    scores = dot_t(q_ref[g, rows, :], key_ref[g * tok + lo : g * tok + hi, :])
    group = count // CHUNK
    token = lax.broadcasted_iota(jnp.int32, (count, hi - lo), 0) // group + t0
    return jnp.where(usable[:, lo:hi] & (token < reach), scores, NEG)


def steps_of(group, h):
    for c in range(h * HALF // CHUNK, (h + 1) * HALF // CHUNK):
        yield c * CHUNK, slice(c * CHUNK * group, (c + 1) * CHUNK * group)


def next_tile(own_ref, q_ref, key_ref, val_ref, acc_in, top_in, acc_ref, top_ref):
    kv, count, hd = q_ref.shape
    tok = val_ref.shape[0] // kv
    group = count // tok
    scale = hd**-0.5 * LOG2E
    usable, reach, _ = reach_of(own_ref, key_ref, tok)
    for h in range(tok // HALF):

        @pl.when(reach > h * HALF)
        def _():
            for t0, rows in steps_of(group, h):
                for g in range(kv):
                    scores = far_scores(q_ref, key_ref, g, rows, t0, reach, usable, 0, tok)
                    old = top_ref[g, rows, :]
                    top = jnp.maximum(old, jnp.max(scores, axis=1, keepdims=True))
                    weights = jnp.exp2((scores - wide(top, scores)) * scale).astype(jnp.bfloat16)
                    shrink = jnp.exp2((old - top) * scale)
                    update = jnp.dot(
                        weights, with_ones(val_ref[g * tok : (g + 1) * tok, :]), preferred_element_type=jnp.float32
                    )
                    acc_ref[g, rows, :] = acc_ref[g, rows, :] * jnp.concatenate([shrink, shrink], axis=1) + update
                    top_ref[g, rows, :] = top


def last_weights(own_ref, q_ref, key_ref, acc_in, top_ref, acc_ref, w_ref):
    kv, count, hd = q_ref.shape
    tok = (key_ref.shape[0] - 8) // kv
    group = count // tok
    scale = hd**-0.5 * LOG2E
    usable, reach, _ = reach_of(own_ref, key_ref, tok)
    for h in range(tok // HALF):
        lo = h * HALF

        @pl.when(reach > lo)
        def _():
            for t0, rows in steps_of(group, h):
                for g in range(kv):
                    scores = far_scores(q_ref, key_ref, g, rows, t0, reach, usable, lo, tok)
                    old = top_ref[g, rows, :]
                    top = jnp.maximum(old, jnp.max(scores, axis=1, keepdims=True))
                    w_ref[g, rows, lo:] = jnp.exp2((scores - wide(top, scores)) * scale).astype(jnp.bfloat16)
                    shrink = jnp.exp2((old - top) * scale)
                    acc_ref[g, rows, :] = acc_ref[g, rows, :] * jnp.concatenate([shrink, shrink], axis=1)


def last_values(own_ref, key_ref, val_ref, w_ref, acc_ref, out_hbm, out_ref, sems):
    tok, heads, hd = out_ref.shape
    kv = acc_ref.shape[0]
    group = heads // kv
    _, reach, _ = reach_of(own_ref, key_ref, tok)
    copies = [
        pltpu.make_async_copy(
            out_ref.at[pl.ds(c * CHUNK, CHUNK)], out_hbm.at[pl.ds(c * CHUNK, CHUNK)], sems.at[c]
        )
        for c in range(tok // CHUNK)
    ]

    def finish(t0, states):
        parts = [(s[:, :hd] / s[:, hd:]).reshape(CHUNK, group, hd) for s in states]
        out_ref[t0 : t0 + CHUNK, :, :] = jnp.concatenate(parts, axis=1).astype(jnp.bfloat16)
        copies[t0 // CHUNK].start()

    for h in range(tok // HALF):
        lo = h * HALF

        @pl.when(reach > lo)
        def _():
            for t0, rows in steps_of(group, h):
                states = []
                for g in range(kv):
                    update = jnp.dot(
                        w_ref[g, rows, lo:],
                        with_ones(val_ref[g * tok + lo : (g + 1) * tok, :]),
                        preferred_element_type=jnp.float32,
                    )
                    states.append(acc_ref[g, rows, :] + update)
                finish(t0, states)

        @pl.when(reach <= lo)
        def _():
            for t0, rows in steps_of(group, h):
                finish(t0, [acc_ref[g, rows, :] for g in range(kv)])

    for copy in copies:
        copy.wait()


def kernel(body, outs, ins, aliases=None, scratch=(), out_specs=None):
    return pl.pallas_call(
        body,
        out_shape=outs,
        in_specs=ins,
        out_specs=out_specs or jax.tree.map(lambda _: VMEM, outs),
        input_output_aliases=aliases or {},
        scratch_shapes=scratch,
        compiler_params=pltpu.CompilerParams(vmem_limit_bytes=LIMIT),
    )


def local(queries, keys, values, seg_ids):
    tok, heads, hd = queries.shape
    kv = keys.shape[1]
    group = heads // kv
    bf16, f32 = jnp.bfloat16, jnp.float32
    struct = jax.ShapeDtypeStruct
    seg_rows = seg_ids.reshape(tok // 128, 128)
    state = (struct((kv, tok * group, 2 * hd), f32), struct((kv, tok * group, 128), f32))
    chunks = tok // CHUNK
    dma = pltpu.SemaphoreType.DMA

    def hop(x, by=1):
        return passed_along(x, by)

    k0, v0 = kernel(
        prepare,
        (struct((kv * tok + 8, hd), bf16), struct((kv * tok, hd), bf16)),
        [HBM] * 3,
        scratch=[
            pltpu.VMEM((tok, kv, hd), bf16),
            pltpu.VMEM((tok, kv, hd), bf16),
            pltpu.VMEM((tok // 128, 128), jnp.int32),
            dma((3,)),
        ],
    )(*(pltpu.with_memory_space_constraint(x, pltpu.HBM) for x in (keys, values, seg_rows)))
    k1, v1 = hop(k0), hop(v0)
    k2, v2 = hop(k1), hop(v1)
    k3, v3 = hop(k2), hop(v2)
    acc, top, q = kernel(
        own_tile,
        (*state, struct((kv, tok * group, hd), bf16)),
        [VMEM] * 3,
        scratch=[pltpu.VMEM((tok, tok), f32)],
    )(queries, k0, v0)
    for kd, vd in ((k1, v1), (k2, v2)):
        acc, top = kernel(next_tile, state, [VMEM] * 6, {4: 0, 5: 1})(k0, q, kd, vd, acc, top)
    acc, weights = kernel(
        last_weights, (state[0], struct((kv, tok * group, tok), bf16)), [VMEM] * 5, {3: 0}
    )(k0, q, k3, acc, top)
    return kernel(
        last_values,
        struct((tok, heads, hd), bf16),
        [VMEM] * 5,
        scratch=[pltpu.VMEM((tok, heads, hd), bf16), dma((chunks,))],
        out_specs=HBM,
    )(k0, k3, v3, weights, acc)


def solution(mesh):
    placed = (P(AXES, "head", None), P(AXES, "head", None), P(AXES, "head", None), P(AXES))
    return jax.shard_map(local, mesh=mesh, in_specs=placed, out_specs=P(AXES, "head", None), check_vma=False)
```

```python
import jax
import jax.numpy as jnp
from jax import lax
from jax.experimental import pallas as pl
from jax.experimental.pallas import tpu as pltpu
from jax.sharding import PartitionSpec as P


AXES = ("dcn", "ctx")
LOG2E = 1.4426950408889634
NEG = -1e30
CHUNK = 64
HALF = 128
LIMIT = 24 * 1024 * 1024

VMEM = pl.BlockSpec(memory_space=pltpu.VMEM)
HBM = pl.BlockSpec(memory_space=pltpu.HBM)


def passed_along(x, crossing=0):
    count, inner = lax.axis_size(AXES), lax.axis_size("ctx")
    if crossing:
        pairs = [(i - crossing, i) for i in range(inner, count, inner)]
    else:
        pairs = [(i, i + 1) for i in range(count - 1) if (i + 1) % inner]
    return lax.ppermute(x, AXES, pairs)


def merge(a_ref, b_ref, out_ref):
    out_ref[...] = (a_ref[...].astype(jnp.float32) + b_ref[...].astype(jnp.float32)).astype(out_ref.dtype)


def prepare(k_hbm, v_hbm, seg_hbm, q_hbm, key_ref, val_ref, raw_ref, k_ref, v_ref, seg_ref, sems):
    tok, kv, _ = k_ref.shape
    rows = seg_ref.shape[0]
    copies = [
        pltpu.make_async_copy(src, dst, sems.at[n])
        for n, (src, dst) in enumerate(((k_hbm, k_ref), (seg_hbm, seg_ref), (v_hbm, v_ref), (q_hbm, raw_ref)))
    ]
    for copy in copies:
        copy.start()

    def pack(src, dst):
        x = src[...].astype(jnp.float32)
        for g in range(kv):
            dst[g * tok : (g + 1) * tok, :] = x[:, g, :].astype(jnp.bfloat16)

    copies[0].wait()
    pack(k_ref, key_ref)
    copies[1].wait()
    marks = (seg_ref[...] + 1).astype(jnp.float32)
    pad = jnp.zeros((8 - rows, 128), jnp.float32)
    key_ref[kv * tok :, :] = jnp.concatenate([marks, pad], axis=0).astype(jnp.bfloat16)
    copies[2].wait()
    pack(v_ref, val_ref)
    copies[3].wait()


def wide(x, like):
    return jnp.concatenate([x] * (like.shape[1] // x.shape[1]), axis=1)


def dot_t(a, b):
    return lax.dot_general(a, b, (((1,), (1,)), ((), ())), preferred_element_type=jnp.float32)


def with_ones(vals):
    return jnp.concatenate([vals, jnp.ones(vals.shape, vals.dtype)], axis=1)


def marks_of(key_ref, tok):
    base = key_ref.shape[0] - 8
    tail = key_ref[base : base + 8, :].astype(jnp.float32)
    return jnp.concatenate([tail[r : r + 1, :] for r in range(tok // 128)], axis=1)


def own_tile(raw_ref, key_ref, val_ref, acc_ref, top_ref, q_ref, bias_ref):
    tok, heads, hd = raw_ref.shape
    kv = acc_ref.shape[0]
    group = heads // kv
    scale = hd**-0.5 * LOG2E
    key_seg = marks_of(key_ref, tok)
    for r in range(tok // 128):
        marks = jnp.broadcast_to(key_seg[:, r * 128 : (r + 1) * 128], (128, 128)).T
        row = lax.broadcasted_iota(jnp.int32, (128, tok), 0) + r * 128
        col = lax.broadcasted_iota(jnp.int32, (128, tok), 1)
        same = jnp.concatenate([marks] * (tok // 128), axis=1) == key_seg
        bias_ref[r * 128 : (r + 1) * 128, :] = jnp.where(same & (col <= row), 0.0, NEG)
    for c in range(tok // CHUNK):
        t0 = c * CHUNK
        width = min(tok, -(-(t0 + CHUNK) // 128) * 128)
        bias = bias_ref[t0 : t0 + CHUNK, :width]
        rows = slice(t0 * group, (t0 + CHUNK) * group)
        raw = raw_ref[t0 : t0 + CHUNK, :, :].astype(jnp.float32)
        for g in range(kv):
            q = raw[:, g * group : (g + 1) * group, :].reshape(CHUNK * group, hd).astype(jnp.bfloat16)
            q_ref[g, rows, :] = q
            scores = dot_t(q, key_ref[g * tok : g * tok + width, :])
            scores = (scores.reshape(CHUNK, group, width) + bias[:, None, :]).reshape(CHUNK * group, width)
            top = jnp.max(scores, axis=1, keepdims=True)
            weights = jnp.exp2((scores - top) * scale).astype(jnp.bfloat16)
            acc_ref[g, rows, :] = jnp.dot(
                weights, with_ones(val_ref[g * tok : g * tok + width, :]), preferred_element_type=jnp.float32
            )
            top_ref[g, rows, :] = jnp.broadcast_to(top, (CHUNK * group, 128))


def reach_of(own_ref, far_ref, tok):
    own = marks_of(own_ref, tok)
    first = own[:, 0:1]
    usable = marks_of(far_ref, tok) == first
    reach = jnp.sum(jnp.where(own == first, 1.0, 0.0)).astype(jnp.int32)
    found = jnp.sum(jnp.where(usable, 1.0, 0.0)).astype(jnp.int32)
    return usable, jnp.where(found > 0, reach, 0), found


def far_scores(q_ref, key_ref, g, rows, t0, reach, usable, lo, hi):
    tok = usable.shape[1]
    count = rows.stop - rows.start
    scores = dot_t(q_ref[g, rows, :], key_ref[g * tok + lo : g * tok + hi, :])
    group = count // CHUNK
    token = lax.broadcasted_iota(jnp.int32, (count, hi - lo), 0) // group + t0
    return jnp.where(usable[:, lo:hi] & (token < reach), scores, NEG)


def steps_of(group, h):
    for c in range(h * HALF // CHUNK, (h + 1) * HALF // CHUNK):
        yield c * CHUNK, slice(c * CHUNK * group, (c + 1) * CHUNK * group)


def next_tile(own_ref, q_ref, key_ref, val_ref, acc_in, top_in, acc_ref, top_ref):
    kv, count, hd = q_ref.shape
    tok = val_ref.shape[0] // kv
    group = count // tok
    scale = hd**-0.5 * LOG2E
    usable, reach, _ = reach_of(own_ref, key_ref, tok)
    for h in range(tok // HALF):

        @pl.when(reach > h * HALF)
        def _():
            for t0, rows in steps_of(group, h):
                for g in range(kv):
                    scores = far_scores(q_ref, key_ref, g, rows, t0, reach, usable, 0, tok)
                    old = top_ref[g, rows, :]
                    top = jnp.maximum(old, jnp.max(scores, axis=1, keepdims=True))
                    weights = jnp.exp2((scores - wide(top, scores)) * scale).astype(jnp.bfloat16)
                    shrink = jnp.exp2((old - top) * scale)
                    update = jnp.dot(
                        weights, with_ones(val_ref[g * tok : (g + 1) * tok, :]), preferred_element_type=jnp.float32
                    )
                    acc_ref[g, rows, :] = acc_ref[g, rows, :] * jnp.concatenate([shrink, shrink], axis=1) + update
                    top_ref[g, rows, :] = top


def out_copies(buf_ref, out_hbm, sems):
    return [
        pltpu.make_async_copy(
            buf_ref.at[pl.ds(c * CHUNK, CHUNK)], out_hbm.at[pl.ds(c * CHUNK, CHUNK)], sems.at[c]
        )
        for c in range(buf_ref.shape[0] // CHUNK)
    ]


def finish(buf_ref, t0, states):
    hd = buf_ref.shape[-1]
    parts = [(s[:, :hd] / s[:, hd:]).reshape(CHUNK, s.shape[0] // CHUNK, hd) for s in states]
    buf_ref[t0 : t0 + CHUNK, :, :] = jnp.concatenate(parts, axis=1).astype(jnp.bfloat16)


def last_weights(own_ref, q_ref, key_ref, acc_in, top_ref, acc_ref, w_ref, out_hbm, buf_ref, sems):
    kv, count, hd = q_ref.shape
    tok = (key_ref.shape[0] - 8) // kv
    group = count // tok
    scale = hd**-0.5 * LOG2E
    usable, reach, _ = reach_of(own_ref, key_ref, tok)
    copies = out_copies(buf_ref, out_hbm, sems)
    halves = tok // HALF
    for h in range(halves):
        lo = h * HALF

        @pl.when(reach > lo)
        def _():
            for t0, rows in steps_of(group, h):
                for g in range(kv):
                    scores = far_scores(q_ref, key_ref, g, rows, t0, reach, usable, lo, tok)
                    old = top_ref[g, rows, :]
                    top = jnp.maximum(old, jnp.max(scores, axis=1, keepdims=True))
                    w_ref[g, rows, lo:] = jnp.exp2((scores - wide(top, scores)) * scale).astype(jnp.bfloat16)
                    shrink = jnp.exp2((old - top) * scale)
                    acc_ref[g, rows, :] = acc_ref[g, rows, :] * jnp.concatenate([shrink, shrink], axis=1)

    for h in range(halves):

        @pl.when((reach <= h * HALF) & (reach > (h - 1) * HALF))
        def _():
            for part in range(h, halves):
                for t0, rows in steps_of(group, part):
                    finish(buf_ref, t0, [acc_ref[g, rows, :] for g in range(kv)])
                    copies[t0 // CHUNK].start()
            for c in range(h * HALF // CHUNK, len(copies)):
                copies[c].wait()


def last_values(own_ref, key_ref, val_ref, w_ref, acc_ref, out_in, out_hbm, buf_ref, sems):
    tok, heads, _ = buf_ref.shape
    kv = acc_ref.shape[0]
    group = heads // kv
    _, reach, _ = reach_of(own_ref, key_ref, tok)
    copies = out_copies(buf_ref, out_hbm, sems)
    halves = tok // HALF
    for top in range(1, halves + 1):

        @pl.when((reach > (top - 1) * HALF) & (reach <= top * HALF))
        def _():
            for h in range(top):
                lo = h * HALF
                for t0, rows in steps_of(group, h):
                    states = []
                    for g in range(kv):
                        update = jnp.dot(
                            w_ref[g, rows, lo:],
                            with_ones(val_ref[g * tok + lo : (g + 1) * tok, :]),
                            preferred_element_type=jnp.float32,
                        )
                        states.append(acc_ref[g, rows, :] + update)
                    finish(buf_ref, t0, states)
                    copies[t0 // CHUNK].start()
            for c in range(top * HALF // CHUNK):
                copies[c].wait()


def kernel(body, outs, ins, aliases=None, scratch=(), out_specs=None):
    return pl.pallas_call(
        body,
        out_shape=outs,
        in_specs=ins,
        out_specs=out_specs or jax.tree.map(lambda _: VMEM, outs),
        input_output_aliases=aliases or {},
        scratch_shapes=scratch,
        compiler_params=pltpu.CompilerParams(vmem_limit_bytes=LIMIT),
    )


def local(queries, keys, values, seg_ids):
    tok, heads, hd = queries.shape
    kv = keys.shape[1]
    group = heads // kv
    bf16, f32 = jnp.bfloat16, jnp.float32
    struct = jax.ShapeDtypeStruct
    seg_rows = seg_ids.reshape(tok // 128, 128)
    state = (struct((kv, tok * group, 2 * hd), f32), struct((kv, tok * group, 128), f32))
    chunks = tok // CHUNK
    dma = pltpu.SemaphoreType.DMA

    def hop(x, crossing=0):
        return passed_along(x, crossing)

    def joined(a, b):
        return kernel(merge, struct(a.shape, a.dtype), [VMEM] * 2)(a, b)

    k0, v0, raw = kernel(
        prepare,
        (struct((kv * tok + 8, hd), bf16), struct((kv * tok, hd), bf16), struct(queries.shape, bf16)),
        [HBM] * 4,
        scratch=[
            pltpu.VMEM((tok, kv, hd), bf16),
            pltpu.VMEM((tok, kv, hd), bf16),
            pltpu.VMEM((tok // 128, 128), jnp.int32),
            dma((4,)),
        ],
    )(*(pltpu.with_memory_space_constraint(x, pltpu.HBM) for x in (keys, values, seg_rows, queries)))
    ki1, kc1 = hop(k0), hop(k0, 1)
    vi1, vc1 = hop(v0), hop(v0, 1)
    kc2, vc2 = hop(ki1, 1), hop(vi1, 1)
    kc3, vc3 = hop(k0, 3), hop(v0, 3)
    k1, v1 = joined(ki1, kc1), joined(vi1, vc1)
    k2, v2 = joined(hop(k1), kc2), joined(hop(v1), vc2)
    k3, v3 = joined(hop(k2), kc3), joined(hop(v2), vc3)
    acc, top, q = kernel(
        own_tile,
        (*state, struct((kv, tok * group, hd), bf16)),
        [VMEM] * 3,
        scratch=[pltpu.VMEM((tok, tok), f32)],
    )(raw, k0, v0)
    for kd, vd in ((k1, v1), (k2, v2)):
        acc, top = kernel(next_tile, state, [VMEM] * 6, {4: 0, 5: 1})(k0, q, kd, vd, acc, top)
    buffers = [pltpu.VMEM((tok, heads, hd), bf16), dma((chunks,))]
    result = struct((tok, heads, hd), bf16)
    acc, weights, out = kernel(
        last_weights,
        (state[0], struct((kv, tok * group, tok), bf16), result),
        [VMEM] * 5,
        {3: 0},
        scratch=buffers,
        out_specs=(VMEM, VMEM, HBM),
    )(k0, q, k3, acc, top)
    return kernel(last_values, result, [VMEM] * 5 + [HBM], {5: 0}, scratch=buffers, out_specs=HBM)(
        k0, k3, v3, weights, acc, out
    )


def solution(mesh):
    placed = (P(AXES, "head", None), P(AXES, "head", None), P(AXES, "head", None), P(AXES))
    return jax.shard_map(local, mesh=mesh, in_specs=placed, out_specs=P(AXES, "head", None), check_vma=False)
```
